256 devices in a mesh: dp: 4 (over y), expert: 64 (over z, x, core).
Axes of the slice: x: 4, y: 4, z: 8, core: 2. Of those that a mesh axis runs over, the one named last changes fastest.
Arguments:
- tokens: bfloat16 [8192, 3584], P('expert', 'dp'), may hold values from -6 to 6
- expert_ids: int32 [8192, 8], P('expert'), may hold values from 0 to 63, as said below
- replica_choice: int32 [8192, 8], P('expert'), may hold values from 0 to 1, as said below
- gate_weights: float32 [8192, 8], P('expert'), may hold values from 0.1 to 1
- placement: int32 [32, 2], replicated, may hold values from 0 to 63, as said below
- capacity: int32 [96], replicated, may hold values from 6 to 12, as said below
- w_gate: bfloat16 [64, 2, 3584, 1024], P('expert', None, 'dp'), as said below
- w_up: bfloat16 [64, 2, 3584, 1024], P('expert', None, 'dp'), as said below
- w_down: bfloat16 [64, 2, 1024, 3584], P('expert', None, None, 'dp'), as said below
Outputs:
- combined: bfloat16 [8192, 3584], P('expert', 'dp')
The draws below stay inside these ranges and needn't reach their ends.
Inputs may be any that keep to these rules, and one draw needn't show every extreme that they name: `expert_ids`: each row names 8 different experts; in every aligned block of 128 rows some hot expert is named by at least 24 rows. `replica_choice`: 1 only where the slot's expert is hot; in every aligned block of 128 rows both replicas of some hot expert whose replicas have capacity 12 receive 12 or more slots. `placement`: column 0 holds 32 different expert numbers; column 1 holds 32 different expert-axis indices, none of them the own index of a hot expert. Entry e below 64 belongs to expert e's own replica, entry 64 + j to the copy of expert placement[j, 0]; both replicas of some hot expert have capacity 12. w_gate[placement[j, 1], 1] equals w_gate[placement[j, 0], 0]; entry [h, 1] is zero where index h hosts no copy. `w_up`: laid out as w_gate. `w_down`: laid out as w_gate.
All inputs are finite; a program needn't handle non-finite values.
Results may differ from the reference program's by a relative error of at most 0.0057.
Values may be sent and summed in bfloat16 or wider, within the bound.
A program may use at most 128 MiB of HBM per device.

```python
import math
import jax
import jax.numpy as jnp
from jax import lax

D = 3584
FF = 1024
TOP = 8
TOK_DEV = 128
EXPERTS = 64
HOT = 32
CAP = 12
TOKENS = 8192


def routing_tables(key):
    base = jax.random.fold_in(key, 4242)
    keys = jax.random.split(base, 6)
    blocks = TOKENS // TOK_DEV
    expert_iota = jnp.arange(EXPERTS, dtype=jnp.int32)
    order = jax.random.permutation(keys[0], EXPERTS).astype(jnp.int32)
    hot_ids = order[:HOT]
    host_ids = order[HOT:2 * HOT]
    placement = jnp.stack([hot_ids, host_ids], 1).astype(jnp.int32)
    bias = jax.random.randint(keys[1], (EXPERTS,), 0, 4096, dtype=jnp.int32)
    noise = jax.random.randint(keys[2], (TOKENS, EXPERTS), 0, 4096, dtype=jnp.int32)
    tie = jax.random.randint(keys[3], (blocks, TOK_DEV), 0, 65536, dtype=jnp.int32)
    keyed = tie * TOK_DEV + jnp.arange(TOK_DEV, dtype=jnp.int32)[None, :]
    first = jnp.argsort(keyed, axis=1, stable=True)
    order_in = jnp.argsort(first, axis=1, stable=True).astype(jnp.int32).reshape(TOKENS)
    forced = order_in < 2 * CAP
    first_hot = hot_ids[0]
    boost = jnp.where(forced[:, None] & (expert_iota[None, :] == first_hot), 16384, 0)
    score = (noise + bias[None, :] + boost) * EXPERTS + expert_iota[None, :]
    _, chosen = lax.top_k(score, TOP)
    expert_ids = chosen.astype(jnp.int32)
    is_hot = jnp.any(expert_ids[:, :, None] == hot_ids[None, None, :], -1)
    coin = jax.random.randint(keys[4], (TOKENS, TOP), 0, 2, dtype=jnp.int32)
    replica = jnp.where(is_hot, coin, 0)
    first_slot = forced[:, None] & (jnp.arange(TOP, dtype=jnp.int32)[None, :] == 0)
    replica = jnp.where(first_slot, (order_in % 2)[:, None], replica).astype(jnp.int32)
    capacity = jax.random.randint(keys[5], (EXPERTS + HOT,), max(1, CAP // 2), CAP + 1, dtype=jnp.int32)
    entry_iota = jnp.arange(EXPERTS + HOT, dtype=jnp.int32)
    capacity = jnp.where((entry_iota == first_hot) | (entry_iota == EXPERTS), CAP, capacity).astype(jnp.int32)
    return (placement, expert_ids, replica, capacity)


def resident_weights(key, which, fan_in, rows, cols):
    placement = routing_tables(key)[0]
    base = jax.random.fold_in(key, 7100 + which)
    own = (jax.random.normal(base, (EXPERTS, rows, cols), jnp.float32) * fan_in ** (-0.5)).astype(jnp.bfloat16)
    device_iota = jnp.arange(EXPERTS, dtype=jnp.int32)
    guest_match = (placement[None, :, 1] == device_iota[:, None]).astype(jnp.int32)
    guest_expert = jnp.sum(guest_match * placement[None, :, 0], 1)
    has_guest = jnp.sum(guest_match, 1) > 0
    guest = jnp.where(has_guest[:, None, None], own[guest_expert], jnp.zeros((), jnp.bfloat16))
    return jnp.stack([own, guest], 1)


def draw_placement(key, part):
    return routing_tables(key)[0]


def draw_expert_ids(key, part):
    return routing_tables(key)[1]


def draw_replica_choice(key, part):
    return routing_tables(key)[2]


def draw_capacity(key, part):
    return routing_tables(key)[3]


def draw_w_gate(key, part):
    return resident_weights(key, 1, D, D, FF)


def draw_w_up(key, part):
    return resident_weights(key, 2, D, D, FF)


def draw_w_down(key, part):
    return resident_weights(key, 3, FF, FF, D)


def shard_levels(key, extent, shards, smallest, high):
    def one(axis_at, parts):
        heights = jax.random.uniform(jax.random.fold_in(jax.random.fold_in(key, 6), axis_at), (parts,), jnp.float32, smallest / len(shards), high / len(shards))
        return jnp.repeat(jnp.exp(heights), extent[axis_at] // parts).reshape((-1,) + (1,) * (len(extent) - axis_at - 1))

    level = one(*shards[0])
    for cut in shards[1:]:
        level = level * one(*cut)
    return level


def normal_values(key, extent, spread, bound, cuts=(), kind=jnp.bfloat16):
    drawn = spread * jax.random.normal(key, extent, jnp.float32)
    if cuts:
        drawn = drawn * shard_levels(key, extent, cuts, -0.22, 0.18)
    return jnp.clip(drawn, -bound, bound).astype(kind)


def setup_inputs(seed: int = 0) -> dict:
    seeds = jax.random.split(jax.random.key(seed), 10)
    return {
        "tokens": normal_values(seeds[0], (TOKENS, D), 1.0, 6.0, ((0, 64), (1, 4))),
        "expert_ids": draw_expert_ids(jax.random.fold_in(seeds[9], 71), 0),
        "replica_choice": draw_replica_choice(jax.random.fold_in(seeds[9], 71), 0),
        "gate_weights": jnp.clip(jnp.exp(math.log(1.0) - 2.3025851 * jax.random.uniform(seeds[3], (TOKENS, TOP), jnp.float32) ** shard_levels(seeds[3], (TOKENS, TOP), ((0, 64),), -0.2, 0.2)), 0.1, 1.0),
        "placement": draw_placement(jax.random.fold_in(seeds[9], 71), 0),
        "capacity": draw_capacity(jax.random.fold_in(seeds[9], 71), 0),
        "w_gate": draw_w_gate(jax.random.fold_in(seeds[9], 71), 0),
        "w_up": draw_w_up(jax.random.fold_in(seeds[9], 71), 0),
        "w_down": draw_w_down(jax.random.fold_in(seeds[9], 71), 0),
    }


def reference(tokens, expert_ids, replica_choice, gate_weights, placement, capacity, w_gate, w_up, w_down):
    blocks = TOKENS // TOK_DEV
    slot_count = TOK_DEV * TOP
    all_slots = TOKENS * TOP
    hot_ids = placement[:, 0]
    flat_ids = expert_ids.reshape(blocks, slot_count)
    flat_rep = replica_choice.reshape(blocks, slot_count)
    hot_match = (flat_ids[:, :, None] == hot_ids[None, None, :]).astype(jnp.int32)
    hot_slot = jnp.sum(hot_match * jnp.arange(HOT, dtype=jnp.int32)[None, None, :], -1)
    target = jnp.where(flat_rep == 1, EXPERTS + hot_slot, flat_ids)
    onehot = (target[:, :, None] == jnp.arange(EXPERTS + HOT, dtype=jnp.int32)[None, None, :]).astype(jnp.int32)
    before = jnp.cumsum(onehot, 1) - onehot
    slot_rank = jnp.sum(before * onehot, -1)
    slot_limit = jnp.sum(onehot * capacity[None, None, :], -1)
    retained = slot_rank < slot_limit
    per_expert = blocks * 2 * CAP
    block_index = jnp.arange(blocks, dtype=jnp.int32)[:, None]
    position = jnp.where(retained, flat_ids * per_expert + (block_index * 2 + flat_rep) * CAP + slot_rank, EXPERTS * per_expert).astype(jnp.int32)
    slot_ids = jnp.arange(all_slots, dtype=jnp.int32)
    table = jnp.full((EXPERTS * per_expert,), all_slots, jnp.int32)
    table = table.at[position.reshape(-1)].set(slot_ids, mode="drop").reshape(EXPERTS, per_expert)
    flat_weights = gate_weights.reshape(-1)

    def one_expert(combined, inputs):
        entries, gate_mat, up_mat, down_mat = inputs
        valid = entries < all_slots
        safe = jnp.minimum(entries, all_slots - 1).astype(jnp.int32)
        token_index = (safe // TOP).astype(jnp.int32)
        token_rows = jnp.where(valid[:, None], tokens[token_index], jnp.zeros((), tokens.dtype))
        gate_part = jnp.dot(token_rows, gate_mat, preferred_element_type=jnp.float32)
        up_part = jnp.dot(token_rows, up_mat, preferred_element_type=jnp.float32)
        hidden = (jax.nn.silu(gate_part) * up_part).astype(jnp.bfloat16)
        result = jnp.dot(hidden, down_mat, preferred_element_type=jnp.float32).astype(jnp.bfloat16)
        scale = jnp.where(valid, flat_weights[safe], jnp.zeros((), jnp.float32))
        combined = combined.at[token_index].add(scale[:, None] * result.astype(jnp.float32))
        return combined, None

    combined, _ = lax.scan(one_expert, jnp.zeros((TOKENS, D), jnp.float32), (table, w_gate[:, 0], w_up[:, 0], w_down[:, 0]))
    return combined.astype(jnp.bfloat16)
```

```python
import jax
import jax.numpy as jnp
from jax import lax
from jax.sharding import PartitionSpec as P


def slot_room(token_count, top_count, expert_count):
    return max(2, min(token_count // 4, 3 * token_count * top_count // (4 * expert_count)))


def on_device(
    tokens, expert_ids, replica_choice, gate_weights, placement, capacity, w_gate, w_up, w_down
):
    expert_count = lax.axis_size("expert")
    token_count, columns = tokens.shape
    top_count = expert_ids.shape[1]
    hot_count = placement.shape[0]
    replicas = expert_count + hot_count
    room_each = slot_room(token_count, top_count, expert_count)
    buffer_slots = expert_count * 2 * room_each
    slot_count = token_count * top_count
    hot_ids = placement[:, 0]
    flat_ids = expert_ids.reshape(-1)
    copy_flag = replica_choice.reshape(-1)
    hot_match = (flat_ids[:, None] == hot_ids[None, :]).astype(jnp.int32)
    hot_slot = jnp.sum(hot_match * jnp.arange(hot_count, dtype=jnp.int32)[None, :], 1)
    target = jnp.where(copy_flag == 1, expert_count + hot_slot, flat_ids)
    onehot = (target[:, None] == jnp.arange(replicas, dtype=jnp.int32)[None, :]).astype(jnp.int32)
    slots = jnp.arange(slot_count, dtype=jnp.int32)
    earlier = (slots[None, :] < slots[:, None]).astype(jnp.bfloat16)
    before = jnp.dot(earlier, onehot.astype(jnp.bfloat16), preferred_element_type=jnp.float32).astype(jnp.int32)
    slot_rank = jnp.sum(before * onehot, 1)
    slot_limit = jnp.sum(onehot * capacity[None, :], 1)
    retained = slot_rank < slot_limit
    own_gate = w_gate[0, 0]
    own_up = w_up[0, 0]
    own_down = w_down[0, 0]
    position = jnp.where(retained, (flat_ids * 2 + copy_flag) * room_each + slot_rank, buffer_slots)
    source = jnp.full((buffer_slots,), slot_count, jnp.int32)
    source = source.at[position].set(jnp.arange(slot_count, dtype=jnp.int32), mode="drop")
    filled = source < slot_count
    token_rows = tokens[jnp.minimum(source, slot_count - 1) // top_count]
    outgoing = jnp.where(filled[:, None], token_rows, jnp.zeros((), tokens.dtype)).reshape(
        expert_count, 2, room_each, columns
    )
    received = lax.all_to_all(outgoing, "expert", split_axis=0, concat_axis=0, tiled=True)
    gate_part = jnp.einsum("nkcd,df->nkcf", received, own_gate, preferred_element_type=jnp.float32)
    up_part = jnp.einsum("nkcd,df->nkcf", received, own_up, preferred_element_type=jnp.float32)
    gate_part, up_part = (
        lax.psum_scatter(gate_part, "dp", scatter_dimension=3, tiled=True),
        lax.psum_scatter(up_part, "dp", scatter_dimension=3, tiled=True),
    )
    hidden = (jax.nn.silu(gate_part) * up_part).astype(jnp.bfloat16)
    hidden = lax.all_gather(hidden, "dp", axis=3, tiled=True)
    result = jnp.einsum("nkcf,fd->nkcd", hidden, own_down, preferred_element_type=jnp.float32)
    result = result.astype(jnp.bfloat16)
    returned = lax.all_to_all(result, "expert", split_axis=0, concat_axis=0, tiled=True)
    returned_flat = returned.reshape(buffer_slots, columns)
    picked = returned_flat[jnp.minimum(position, buffer_slots - 1)]
    weight = jnp.where(retained, gate_weights.reshape(-1), jnp.zeros((), jnp.float32))
    combined = jnp.sum(
        (weight[:, None] * picked.astype(jnp.float32)).reshape(token_count, top_count, columns), 1
    )
    return combined.astype(jnp.bfloat16)


def solution(mesh):
    return jax.shard_map(
        on_device,
        mesh=mesh,
        in_specs=(
            P("expert", "dp"),
            P("expert", None),
            P("expert", None),
            P("expert", None),
            P(),
            P(),
            P("expert", None, "dp", None),
            P("expert", None, "dp", None),
            P("expert", None, None, "dp"),
        ),
        out_specs=P("expert", "dp"),
        check_vma=False,
    )
```

```python
import functools

import jax
import jax.numpy as jnp
from jax import lax
from jax.experimental import pallas as pl
from jax.experimental.pallas import tpu as pltpu
from jax.sharding import PartitionSpec as P

MESH = pl.DeviceIdType.MESH
F32 = jnp.float32
BF16 = jnp.bfloat16
I32 = jnp.int32
LANES = 128
CODE = 64

SIZES = dict(nz=8, nx=4, nc=2, cap=12)


def kernel(
    cfg,
    tok_ref, ids_ref, rep_ref, gw_ref, place_ref, place_s, cap_ref, wg_hbm, wu_hbm, wd_hbm,
    out_ref,
    wg, wu, wd, w_sem,
    tokg, metag, zt_send, zt_recv, zm_send, zm_recv,
    sel, xsend, xrecv, x_ssem, x_rsem,
    part, r1s, r1r, r2s, r2r, hid, r1_ssem, r1_rsem, r2_ssem, r2_rsem,
    a1_ssem, a1_rsem, a2_ssem, a2_rsem,
    osend, oret, o_ssem, o_rsem, o_lsem,
    acc, csend, crecv, c_ssem, c_rsem,
):
    nz, nx, nc, cap = cfg["nz"], cfg["nx"], cfg["nc"], cfg["cap"]
    half = cap // 2
    experts = nz * nx * nc
    hot = place_ref.shape[0]
    top = ids_ref.shape[0]
    tb, cols = tok_ref.shape
    zs = nz // 2
    slots = nx * nc
    ar, br = zs * cap, zs * half
    bp = -(-br // 16) * 16
    rr = ar + bp
    ua, ub = nc * ar, nc * br
    ur = ua + ub
    units = 2 * nx

    y = lax.axis_index("dp")
    e = lax.axis_index("expert")
    z = e // slots
    x = (e // nc) % nx
    c = e % nc

    def dev(yy, zz, xx, cc):
        return (yy, (zz * nx + xx) * nc + cc)

    z_up = lax.rem(z + 1, nz)
    z_dn = lax.rem(z + nz - 1, nz)
    right = dev(y, z_up, x, c)
    left = dev(y, z_dn, x, c)
    y1 = y + 1 - 2 * (y % 2)
    y2 = 3 - y
    odd, high = y % 2, y // 2
    mate1 = dev(y1, z, x, c)
    mate2 = dev(y2, z, x, c)
    first_mate = (mate1, mate2)
    second_mate = (mate2, mate1)
    keep_half = ((odd + high) % 2, high)
    keep_quarter = (high, odd)

    def slot_dest(s):
        dx, dc = s // nc, s % nc
        return lax.rem(x + dx, nx), lax.rem(c + dc, nc)

    def slot_source(s):
        dx, dc = s // nc, s % nc
        return lax.rem(x + nx - dx, nx), lax.rem(c + nc - dc, nc)

    loads = [
        pltpu.make_async_copy(h.at[0], v, w_sem.at[i])
        for i, (h, v) in enumerate(((wg_hbm, wg), (wu_hbm, wu), (wd_hbm, wd)))
    ]
    for ld in loads:
        ld.start()

    barrier = pltpu.get_barrier_semaphore()
    peers = [right, left, mate1, mate2]
    for s in range(1, slots):
        xx, cc = slot_dest(s)
        peers.append(dev(y, z, xx, cc))
    for peer in peers:
        pl.semaphore_signal(barrier, inc=1, device_id=peer, device_id_type=MESH)
    pl.semaphore_wait(barrier, len(peers))

    def remote(src, dst, ssem, rsem, device):
        return pltpu.make_async_remote_copy(
            src_ref=src, dst_ref=dst, send_sem=ssem, recv_sem=rsem,
            device_id=device, device_id_type=MESH,
        )

    offset = [0]
    for d in range(1, zs + 1):
        offset.append(-d)
        if d < zs:
            offset.append(d)
    entry = {d: n for n, d in enumerate(offset)}
    hops_r, hops_l = zs, zs - 1

    def z_copy(to_right, h, meta):
        sign = -1 if to_right else 1
        src = entry[sign * (h - 1)] if h > 1 else 0
        dst = entry[sign * h]
        i = (h - 1) if to_right else hops_r + (h - 1)
        ref, ss, rs = (metag, zm_send, zm_recv) if meta else (tokg, zt_send, zt_recv)
        source = tok_ref if (h == 1 and not meta) else ref.at[src]
        return remote(source, ref.at[dst], ss.at[i], rs.at[i], right if to_right else left)

    z_copy(True, 1, False).start()
    if hops_l:
        z_copy(False, 1, False).start()

    def iota(shape, dim):
        return lax.broadcasted_iota(I32, shape, dim)

    hot_col = place_ref[:, 0:1]
    host_col = place_ref[:, 1:2]
    reps = experts + hot
    r_iota = iota((reps, tb), 0)
    j_iota = iota((hot, tb), 0)
    targets = []
    chosen = jnp.zeros((reps, tb), F32)
    for k in range(top):
        idk = ids_ref[k : k + 1, :]
        j = jnp.sum(jnp.where(hot_col == idk, j_iota, 0), axis=0, keepdims=True)
        t = jnp.where(rep_ref[k : k + 1, :] == 1, experts + j, idk)
        targets.append(t)
        chosen = chosen + jnp.where(r_iota == t, 1.0, 0.0)
    earlier = jnp.where(iota((tb, tb), 0) < iota((tb, tb), 1), 1.0, 0.0).astype(BF16)
    rank = jnp.dot(chosen.astype(BF16), earlier, preferred_element_type=F32).astype(I32)
    own_code = r_iota[:experts] * CODE + rank[:experts]
    rank_c = rank[experts:]
    copy_code = jnp.where(
        rank_c < half,
        hot_col * CODE + cap + rank_c,
        host_col * CODE + (cap - half) + rank_c,
    )
    code = jnp.concatenate([own_code, copy_code], axis=0)
    code = jnp.where(rank < cap_ref[...], code, -1)
    for k in range(top):
        row = jnp.sum(jnp.where(r_iota == targets[k], code, 0), axis=0, keepdims=True)
        metag[0, k : k + 1, :] = row.astype(F32)
        metag[0, top + k : top + k + 1, :] = gw_ref[k : k + 1, :]
    tokg[0] = tok_ref[...]

    role = jnp.int32(0)
    for j in range(hot):
        role = jnp.maximum(role, jnp.where(place_s[j, 1] == e, 1, 0))

    z_copy(True, 1, True).start()
    if hops_l:
        z_copy(False, 1, True).start()

    def z_relay(h):
        for to_right, hops in ((True, hops_r), (False, hops_l)):
            if h <= hops:
                for meta in (False, True):
                    z_copy(to_right, h, meta).wait_recv()
                    if h < hops:
                        z_copy(to_right, h + 1, meta).start()

    p_iota = iota((rr, 1), 0)
    block_of = jnp.full((rr, 1), -1, I32)
    local = jnp.zeros((rr, 1), I32)
    for i in range(zs):
        in_a = (p_iota >= i * cap) & (p_iota < (i + 1) * cap)
        block_of = jnp.where(in_a, i, block_of)
        local = jnp.where(in_a, p_iota - i * cap, local)
        in_b = (p_iota >= ar + i * half) & (p_iota < ar + (i + 1) * half)
        block_of = jnp.where(in_b, i, block_of)
        local = jnp.where(in_b, p_iota - ar - i * half + cap, local)

    def slot_key(s):
        xx, cc = slot_dest(s)
        return ((z * nx + xx) * nc + cc) * CODE + local

    def x_copy(q, s):
        xx, cc = slot_dest(s)
        return remote(
            xsend.at[q, s], xrecv.at[q, s], x_ssem.at[q, s], x_rsem.at[q, s], dev(y, z, xx, cc)
        )

    def dispatch(q):
        def one(s):
            key = slot_key(s)
            for i in range(zs):
                want = jnp.where(block_of == i, key, -2).astype(F32)
                hit = jnp.zeros((rr, tb), jnp.bool_)
                for k in range(top):
                    hit = hit | (metag[q * zs + i, k : k + 1, :] == want)
                sel[:, i * tb : (i + 1) * tb] = jnp.where(hit, 1.0, 0.0).astype(BF16)
            toks = tokg[q * zs : (q + 1) * zs].reshape(zs * tb, cols)
            return jnp.dot(sel[...], toks, preferred_element_type=F32).astype(BF16)

        xrecv[q, 0] = one(0)

        def body(s, carry):
            xsend[q, s] = one(s)
            x_copy(q, s).start()
            return carry

        lax.fori_loop(1, slots, body, 0)

    def unit(u):
        q = u // nx
        n = u % nx
        return q, (n + n // 2) % nx if nx <= 2 else n + n // 2 - 2 * (n // 3)

    def y_copy(stage, u, ab):
        if stage == 0:
            return remote(r1s.at[u, ab], r1r.at[u, ab], r1_ssem.at[u, ab], r1_rsem.at[u, ab], first_mate[ab])
        if stage == 1:
            return remote(r2s.at[u, ab], r2r.at[u, ab], r2_ssem.at[u, ab], r2_rsem.at[u, ab], second_mate[ab])
        if stage == 2:
            ref = hid.at[u, pl.ds(4 * ab + 2 * keep_half[ab] + keep_quarter[ab], 1)]
            return remote(ref, ref, a1_ssem.at[u, ab], a1_rsem.at[u, ab], second_mate[ab])
        ref = hid.at[u, pl.ds(4 * ab + 2 * keep_half[ab], 2)]
        return remote(ref, ref, a2_ssem.at[u, ab], a2_rsem.at[u, ab], first_mate[ab])

    def y_recv(stage, u, ab):
        if stage < 2:
            y_copy(stage, u, ab).wait_recv()
        elif stage == 2:
            ref = hid.at[u, pl.ds(4 * ab + 2 * keep_half[ab] + 1 - keep_quarter[ab], 1)]
            remote(ref, ref, a1_ssem.at[u, ab], a1_rsem.at[u, ab], second_mate[ab]).wait_recv()
        else:
            ref = hid.at[u, pl.ds(4 * ab + 2 * (1 - keep_half[ab]), 2)]
            remote(ref, ref, a2_ssem.at[u, ab], a2_rsem.at[u, ab], first_mate[ab]).wait_recv()

    def stage_up(u):
        q, dx = unit(u)

        @pl.when(dx > 0)
        def _():
            x_copy(q, nc * dx).wait_recv()

        for dc in range(1, nc):
            x_copy(q, nc * dx + dc).wait_recv()

        def block(b):
            at = pl.ds(pl.multiple_of(b * LANES, LANES), LANES)
            xa = xrecv[q, pl.ds(nc * dx, nc), 0:ar, :].reshape(ua, cols)
            xb = xrecv[q, pl.ds(nc * dx, nc), ar:rr, :].reshape(nc * bp, cols)
            wa = jnp.concatenate([wg[0, :, at], wu[0, :, at]], axis=1)
            wb = jnp.concatenate([wg[role, :, at], wu[role, :, at]], axis=1)
            ya = jnp.dot(xa, wa, preferred_element_type=F32)
            yb = jnp.dot(xb, wb, preferred_element_type=F32)
            yb = yb.reshape(nc, bp, 2 * LANES)[:, :br].reshape(ub, 2 * LANES)
            return jnp.concatenate([ya, yb], axis=0)

        for ab in range(2):

            def send(j, carry, ab=ab):
                r1s[u, ab, j] = block(4 * ab + 2 * (1 - keep_half[ab]) + j).astype(BF16)
                return carry

            lax.fori_loop(0, 2, send, 0)
            y_copy(0, u, ab).start()
        for ab in range(2):

            def keep(j, carry, ab=ab):
                part[u, ab, j] = block(4 * ab + 2 * keep_half[ab] + j)
                return carry

            lax.fori_loop(0, 2, keep, 0)

    def stage_sum(u):
        for ab in range(2):
            y_recv(0, u, ab)
            mine, other = keep_quarter[ab], 1 - keep_quarter[ab]
            r2s[u, ab] = (part[u, ab, other] + r1r[u, ab, other].astype(F32)).astype(BF16)
            y_copy(1, u, ab).start()
            part[u, ab, mine] = part[u, ab, mine] + r1r[u, ab, mine].astype(F32)

    def stage_act(u):
        for ab in range(2):
            y_recv(1, u, ab)
            v = part[u, ab, keep_quarter[ab]] + r2r[u, ab].astype(F32)
            gate, up = v[:, :LANES], v[:, LANES:]
            hidden = gate / (1.0 + jnp.exp(-gate)) * up
            hid[u, 4 * ab + 2 * keep_half[ab] + keep_quarter[ab]] = hidden.astype(BF16)
            y_copy(2, u, ab).start()

    def stage_pass(u):
        for ab in range(2):
            y_recv(2, u, ab)
            y_copy(3, u, ab).start()

    def o_copy(q, s):
        xx, cc = slot_source(s)
        return remote(
            osend.at[q, s], oret.at[q, s], o_ssem.at[q, s], o_rsem.at[q, s], dev(y, z, xx, cc)
        )

    def o_local(q):
        return pltpu.make_async_copy(osend.at[q, 0], oret.at[q, 0], o_lsem.at[q])

    def stage_down(u):
        q, dx = unit(u)
        for ab in range(2):
            y_recv(3, u, ab)
        h = jnp.concatenate([hid[u, b] for b in range(8)], axis=1)
        da = jnp.dot(h[:ua], wd[0], preferred_element_type=F32)
        db = jnp.dot(h[ua:], wd[role], preferred_element_type=F32)
        db = db.reshape(nc, br, cols)
        if bp > br:
            db = jnp.concatenate([db, jnp.zeros((nc, bp - br, cols), F32)], axis=1)
        osend[q, pl.ds(nc * dx, nc), 0:ar, :] = da.astype(BF16).reshape(nc, ar, cols)
        osend[q, pl.ds(nc * dx, nc), ar:rr, :] = db.astype(BF16)

        @pl.when(dx == 0)
        def _():
            o_local(q).start()

        @pl.when(dx > 0)
        def _():
            o_copy(q, nc * dx).start()

        for dc in range(1, nc):
            o_copy(q, nc * dx + dc).start()

    def combine(q):
        o_local(q).wait()

        def arrived(s, carry):
            o_copy(q, s).wait_recv()
            return carry

        lax.fori_loop(1, slots, arrived, 0)

        def one(i, carry):
            total = jnp.zeros((tb, cols), F32)
            keys = jnp.concatenate([jnp.where(block_of == i, slot_key(s), -2) for s in range(slots)], axis=0)
            keys = keys.astype(F32)
            w = jnp.zeros((slots * rr, tb), F32)
            for k in range(top):
                hit = metag[q * zs + i, k : k + 1, :] == keys
                w = w + jnp.where(hit, metag[q * zs + i, top + k : top + k + 1, :], 0.0)
            w_hi = w.astype(BF16)
            w_lo = (w - w_hi.astype(F32)).astype(BF16)
            rows = oret[q].reshape(slots * rr, cols)
            dims = (((0,), (0,)), ((), ()))
            total = lax.dot_general(w_hi, rows, dims, preferred_element_type=F32)
            total = total + lax.dot_general(w_lo, rows, dims, preferred_element_type=F32)
            acc[q * zs + i] = total
            return carry

        lax.fori_loop(0, zs, one, 0)

    z_done = 0
    for h in range(1, zs // 2 + 1):
        z_relay(h)
    dispatch(0)
    for ld in loads:
        ld.wait()

    def step(n):
        def when(stage, lag):
            u = n - lag

            @pl.when((u >= 0) & (u < units))
            def _():
                stage(u)

        when(stage_up, 0)
        when(stage_sum, 1)
        when(stage_act, 2)
        when(stage_pass, 3)
        when(stage_down, 4)

    def steps(lo, hi):
        def body(n, carry):
            step(n)
            return carry

        lax.fori_loop(lo, hi, body, 0)

    steps(0, nx // 2)
    for h in range(zs // 2 + 1, zs + 1):
        z_relay(h)
    dispatch(1)
    steps(nx // 2, nx + 4)
    combine(0)
    steps(nx + 4, units + 4)
    combine(1)

    def c_copy(to_right, h):
        i = (h - 1) if to_right else hops_r + (h - 1)
        return remote(csend.at[i], crecv.at[i], c_ssem.at[i], c_rsem.at[i], right if to_right else left)

    far = entry[-zs]
    for h in range(1, hops_r + 1):
        for to_right, hops in ((True, hops_r), (False, hops_l)):
            if h > hops:
                continue
            d = hops - h + 1
            i = (h - 1) if to_right else hops_r + (h - 1)
            n = entry[d if to_right else -d] if d < zs else far
            v = acc[n]
            if h > 1:
                c_copy(to_right, h - 1).wait_recv()
                v = v + crecv[i - 1].astype(F32)
            csend[i] = v.astype(BF16)
            c_copy(to_right, h).start()
    v = acc[0]
    for to_right, hops in ((False, hops_l), (True, hops_r)):
        if hops:
            c_copy(to_right, hops).wait_recv()
            v = v + crecv[(hops - 1) if to_right else hops_r + hops - 1].astype(F32)
    out_ref[...] = v.astype(BF16)

    for to_right, hops in ((True, hops_r), (False, hops_l)):
        for h in range(1, hops + 1):
            z_copy(to_right, h, False).wait_send()
            z_copy(to_right, h, True).wait_send()
            c_copy(to_right, h).wait_send()

    for q in range(2):

        def sent(s, carry, q=q):
            x_copy(q, s).wait_send()
            o_copy(q, s).wait_send()
            return carry

        lax.fori_loop(1, slots, sent, 0)

    def sent_y(u, carry):
        for ab in range(2):
            for stage in range(4):
                y_copy(stage, u, ab).wait_send()
        return carry

    lax.fori_loop(0, units, sent_y, 0)


def on_device(
    cfg, tokens, expert_ids, replica_choice, gate_weights, placement, capacity, w_gate, w_up, w_down
):
    nz, nx, nc, cap = cfg["nz"], cfg["nx"], cfg["nc"], cfg["cap"]
    tb, cols = tokens.shape
    top = expert_ids.shape[1]
    ff = w_gate.shape[-1]
    zs = nz // 2
    slots = nx * nc
    ar, br = zs * cap, zs * (cap // 2)
    rr = ar + -(-br // 16) * 16
    ur = nc * (ar + br)
    units = 2 * nx
    hops = nz - 1
    vmem = pl.BlockSpec(memory_space=pltpu.VMEM)
    smem = pl.BlockSpec(memory_space=pltpu.SMEM)
    anywhere = pl.BlockSpec(memory_space=pl.ANY)
    dma = pltpu.SemaphoreType.DMA
    assert ff == 8 * LANES
    scratch = [
        pltpu.VMEM((2, cols, ff), BF16), pltpu.VMEM((2, cols, ff), BF16), pltpu.VMEM((2, ff, cols), BF16), dma((3,)),
        pltpu.VMEM((nz, tb, cols), BF16), pltpu.VMEM((nz, 2 * top, tb), F32),
        dma((hops,)), dma((hops,)), dma((hops,)), dma((hops,)),
        pltpu.VMEM((rr, zs * tb), BF16),
        pltpu.VMEM((2, slots, rr, cols), BF16), pltpu.VMEM((2, slots, rr, cols), BF16), dma((2, slots)), dma((2, slots)),
        pltpu.VMEM((units, 2, 2, ur, 2 * LANES), F32),
        pltpu.VMEM((units, 2, 2, ur, 2 * LANES), BF16), pltpu.VMEM((units, 2, 2, ur, 2 * LANES), BF16),
        pltpu.VMEM((units, 2, ur, 2 * LANES), BF16), pltpu.VMEM((units, 2, ur, 2 * LANES), BF16),
        pltpu.VMEM((units, 8, ur, LANES), BF16),
    ]
    scratch += [dma((units, 2)) for _ in range(8)]
    scratch += [
        pltpu.VMEM((2, slots, rr, cols), BF16), pltpu.VMEM((2, slots, rr, cols), BF16),
        dma((2, slots)), dma((2, slots)), dma((2,)),
        pltpu.VMEM((nz, tb, cols), F32),
        pltpu.VMEM((hops, tb, cols), BF16), pltpu.VMEM((hops, tb, cols), BF16), dma((hops,)), dma((hops,)),
    ]
    return pl.pallas_call(
        functools.partial(kernel, cfg),
        out_shape=jax.ShapeDtypeStruct((tb, cols), BF16),
        in_specs=[vmem, vmem, vmem, vmem, vmem, smem, vmem, anywhere, anywhere, anywhere],
        out_specs=vmem,
        scratch_shapes=scratch,
        compiler_params=pltpu.CompilerParams(
            collective_id=0, has_side_effects=True, vmem_limit_bytes=58 * 2**20
        ),
    )(
        tokens, expert_ids.T, replica_choice.T, gate_weights.T, placement, placement,
        capacity.reshape(-1, 1), w_gate, w_up, w_down,
    )


def solution(mesh, cfg=None):
    return jax.shard_map(
        functools.partial(on_device, cfg or SIZES),
        mesh=mesh,
        in_specs=(
            P("expert", "dp"),
            P("expert", None),
            P("expert", None),
            P("expert", None),
            P(),
            P(),
            P("expert", None, "dp", None),
            P("expert", None, "dp", None),
            P("expert", None, None, "dp"),
        ),
        out_specs=P("expert", "dp"),
        check_vma=False,
    )
```

```python
import functools

import jax
import jax.numpy as jnp
from jax import lax
from jax.experimental import pallas as pl
from jax.experimental.pallas import tpu as pltpu
from jax.sharding import PartitionSpec as P

MESH = pl.DeviceIdType.MESH
F32 = jnp.float32
BF16 = jnp.bfloat16
I32 = jnp.int32
LANES = 128
CODE = 64
ALIGN = 8

SIZES = dict(
    nz=8, nx=4, nc=2, cap=12,
    groups=((0,), (1, -1), (2, -2), (3, -3), (4,)),
    order=(0, 1, -2, 4, 3, -3, 2, -1),
    returns=((0, 1), (-2, 4), (3,), (-3,), (2,), (-1,)),
    early=(
        "d0 r10 r11 d1", "w a0 u0 r20", "s0 r21 d2 c0", "r30 a1 u1 r31", "d3 p0 s1 r40", "a2 u2 r41 d4", "c1 s2",
    ),
    begin=(3, 3, 2, 1, 0),
    before={3: "a4", 4: "a3"},
    after={5: "o0", 7: "o1 m0", 8: "o2 m1 R1", 9: "o3 m2 R2", 10: "o4 m3 L1", 11: "o5 L2"},
    late=("m4 R3 m5", "L3 R4"),
)


def room(cfg, blocks):
    return -(-blocks * (cfg["cap"] + cfg["cap"] // 2) // ALIGN) * ALIGN


def kernel(cfg, *refs):
    groups, order, returns = cfg["groups"], cfg["order"], cfg["returns"]
    ng, nr = len(groups), len(returns)
    refs = list(refs)

    def take(n):
        out = refs[:n]
        del refs[:n]
        return out

    tok_ref, ids_ref, rep_ref, gw_ref, place_ref, place_s, cap_ref, wg_hbm, wu_hbm, wd_hbm = take(10)
    (out_ref,) = take(1)
    wg, wu, wd, w_sem = take(4)
    tokg, codes, z_ssem, z_rsem = take(4)
    xs, xr = take(ng), take(ng)
    x_ssem, x_rsem, xc = take(3)
    part, r1s, r1r, r2s, r2r, hid, res = take(7)
    r1_ssem, r1_rsem, r2_ssem, r2_rsem, a1_ssem, a1_rsem, a2_ssem, a2_rsem = take(8)
    os_, or_ = take(nr), take(nr)
    o_ssem, o_rsem = take(2)
    acc, csend, crecv, c_ssem, c_rsem = take(5)
    assert not refs

    nz, nx, nc, cap = cfg["nz"], cfg["nx"], cfg["nc"], cfg["cap"]
    half = cap // 2
    each = cap + half
    experts = nz * nx * nc
    hot = place_ref.shape[1]
    top = ids_ref.shape[0]
    tb, cols = tok_ref.shape
    far = nz // 2
    slots = nx * nc
    ua, ub = slots * cap, slots * half
    ur = ua + ub
    units = nz
    flat = [b for g in groups for b in g]
    entry = {b: i for i, b in enumerate(flat)}
    place_of = {b: i for i, b in enumerate(order)}

    y = lax.axis_index("dp")
    e = lax.axis_index("expert")
    z = e // slots
    x = (e // nc) % nx
    c = e % nc

    def dev(yy, zz, xx, cc):
        return (yy, (zz * nx + xx) * nc + cc)

    right = dev(y, lax.rem(z + 1, nz), x, c)
    left = dev(y, lax.rem(z + nz - 1, nz), x, c)
    odd, high = y % 2, y // 2
    mate1 = dev(y + 1 - 2 * odd, z, x, c)
    mate2 = dev(3 - y, z, x, c)
    first_mate = (mate1, mate2)
    second_mate = (mate2, mate1)
    keep_half = ((odd + high) % 2, high)
    keep_quarter = (high, odd)

    def slot_dest(s):
        dx, dc = s // nc, s % nc
        return lax.rem(x + dx, nx), lax.rem(c + dc, nc)

    def slot_source(s):
        dx, dc = s // nc, s % nc
        return lax.rem(x + nx - dx, nx), lax.rem(c + nc - dc, nc)

    loads = [
        pltpu.make_async_copy(h.at[0], v, w_sem.at[i])
        for i, (h, v) in enumerate(((wg_hbm, wg), (wu_hbm, wu), (wd_hbm, wd)))
    ]
    for ld in loads:
        ld.start()

    barrier = pltpu.get_barrier_semaphore()
    peers = [right, left, mate1, mate2]
    for s in range(1, slots):
        peers.append(dev(y, z, *slot_dest(s)))
    for peer in peers:
        pl.semaphore_signal(barrier, inc=1, device_id=peer, device_id_type=MESH)
    pl.semaphore_wait(barrier, len(peers))

    def remote(src, dst, ssem, rsem, device):
        return pltpu.make_async_remote_copy(
            src_ref=src, dst_ref=dst, send_sem=ssem, recv_sem=rsem,
            device_id=device, device_id_type=MESH,
        )

    pieces = ((0, tb // 2), (tb // 2, tb // 2 + 2 * top))

    def z_hops(to_right, piece):
        return far if to_right == (piece == 0) else far - 1

    def z_copy(to_right, h, piece):
        sign = -1 if to_right else 1

        def at(hops):
            return entry[far if hops == far else sign * hops]

        rows = pl.ds(*pieces[piece])
        source = tok_ref.at[rows] if (h == 1 and piece == 0) else tokg.at[at(h - 1), rows]
        d = 0 if to_right else 1
        return remote(
            source, tokg.at[at(h), rows], z_ssem.at[d, piece, h - 1], z_rsem.at[d, piece, h - 1],
            right if to_right else left,
        )

    def z_start(h, piece):
        for to_right in (True, False):
            if h <= z_hops(to_right, piece):
                z_copy(to_right, h, piece).start()

    def relay(h, piece):
        for to_right in (True, False):
            if h <= z_hops(to_right, piece):
                z_copy(to_right, h, piece).wait_recv()
                if h < z_hops(to_right, piece):
                    z_copy(to_right, h + 1, piece).start()

    z_start(1, 0)

    def iota(shape, dim):
        return lax.broadcasted_iota(I32, shape, dim)

    def column(row):
        n = row.shape[1]
        return jnp.sum(jnp.where(iota((n, n), 0) == iota((n, n), 1), row, 0), axis=1, keepdims=True)

    reps = experts + hot
    hot_col = column(place_ref[0:1, :])
    host_col = column(place_ref[1:2, :])
    cap_col = column(cap_ref[...])
    r_iota = iota((reps, tb), 0)
    j_iota = iota((hot, tb), 0)
    targets = []
    chosen = jnp.zeros((reps, tb), F32)
    for k in range(top):
        idk = ids_ref[k : k + 1, :]
        j = jnp.sum(jnp.where(hot_col == idk, j_iota, 0), axis=0, keepdims=True)
        t = jnp.where(rep_ref[k : k + 1, :] == 1, experts + j, idk)
        targets.append(t)
        chosen = chosen + jnp.where(r_iota == t, 1.0, 0.0)
    earlier = jnp.where(iota((tb, tb), 0) < iota((tb, tb), 1), 1.0, 0.0).astype(BF16)
    rank = jnp.dot(chosen.astype(BF16), earlier, preferred_element_type=F32).astype(I32)
    own_code = r_iota[:experts] * CODE + rank[:experts]
    rank_c = rank[experts:]
    copy_code = jnp.where(
        rank_c < half,
        hot_col * CODE + cap + rank_c,
        host_col * CODE + (cap - half) + rank_c,
    )
    code = jnp.concatenate([own_code, copy_code], axis=0)
    code = jnp.where(rank < cap_col, code, -CODE)
    rows = [
        jnp.sum(jnp.where(r_iota == targets[k], code, 0), axis=0, keepdims=True) for k in range(top)
    ]
    code = jnp.concatenate(rows, axis=0)
    whose = jnp.right_shift(code, 6)
    gw = gw_ref[...]
    gw_hi = gw.astype(BF16)
    gw_lo = (gw - gw_hi.astype(F32)).astype(BF16)
    tail = (whose.astype(F32).astype(BF16), (code - whose * CODE).astype(F32).astype(BF16), gw_hi, gw_lo)
    tokg[0, tb:] = jnp.zeros((2 * top, cols), BF16)
    for i, t in enumerate(tail):
        tokg[0, tb : tb + top, i * tb : (i + 1) * tb] = t
    tokg[0, :tb] = tok_ref[...]
    z_start(1, 1)

    role = jnp.int32(0)
    for j in range(hot):
        role = jnp.maximum(role, jnp.where(place_s[1, j] == e, 1, 0))

    def read_codes(n):
        t = tokg[n, tb : tb + top, 0 : 4 * tb].astype(F32)
        codes[n, 0] = t[:, :tb] * CODE + t[:, tb : 2 * tb]
        codes[n, 1] = t[:, 2 * tb : 3 * tb]
        codes[n, 2] = t[:, 3 * tb :]

    def layout(rr, blocks):
        p = iota((rr, 1), 0)
        block_of = jnp.zeros((rr, 1), I32)
        for i in range(1, blocks + 1):
            block_of = block_of + jnp.where(p >= i * each, 1, 0)
        return block_of, p - block_of * each

    def slot_keys(rr, blocks, i, source):
        block_of, local = layout(rr, blocks)
        keys = []
        for s in range(slots):
            xx, cc = slot_dest(s)
            key = ((z * nx + xx) * nc + cc) * CODE + local
            keys.append(jnp.where(block_of == i, key, -2))
        return jnp.concatenate(keys, axis=0).astype(F32)

    def x_copy(g, s):
        xx, cc = slot_dest(s)
        return remote(xs[g].at[s], xr[g].at[s], x_ssem.at[g, s], x_rsem.at[g, s], dev(y, z, xx, cc))

    def loop(lo, hi, f):
        def body(i, carry):
            f(i)
            return carry

        lax.fori_loop(lo, hi, body, 0)

    def dispatch(g):
        blocks = groups[g]
        nb = len(blocks)
        rr = room(cfg, nb)
        n0 = entry[blocks[0]]
        sel = []
        for i in range(nb):
            read_codes(n0 + i)
            keys = slot_keys(rr, nb, i, False)
            hit = jnp.zeros((slots * rr, tb), jnp.bool_)
            for k in range(top):
                hit = hit | (codes[n0 + i, 0, k : k + 1, :] == keys)
            sel.append(jnp.where(hit, 1.0, 0.0).astype(BF16))
        sel = jnp.concatenate(sel, axis=1)
        toks = tokg[n0 : n0 + nb, :tb].reshape(nb * tb, cols)
        picked = jnp.dot(sel, toks, preferred_element_type=F32)
        xs[g][...] = picked.reshape(slots, rr, cols).astype(BF16)
        loop(1, slots, lambda s: x_copy(g, s).start())
        xr[g][0] = picked[0:rr].astype(BF16)

    def joined(ref):
        return ref[...].astype(F32).reshape(slots * ref.shape[1], cols).astype(BF16)

    def unit_rows(rr, i):
        p = iota((ur, 1), 0)
        s = jnp.zeros((ur, 1), I32)
        for j in range(1, slots):
            s = s + jnp.where(p >= j * cap, 1, 0) * jnp.where(p < ua, 1, 0)
            s = s + jnp.where(p >= ua + j * half, 1, 0)
        local = jnp.where(p < ua, p - s * cap, p - ua - s * half + cap)
        return s * rr + i * each + local

    def arrive(g):
        blocks = groups[g]
        rr = room(cfg, len(blocks))
        loop(1, slots, lambda s: x_copy(g, s).wait_recv())
        rows = joined(xr[g])
        for i, b in enumerate(blocks):
            perm = jnp.where(unit_rows(rr, i) == iota((ur, slots * rr), 1), 1.0, 0.0).astype(BF16)
            xc[place_of[b]] = jnp.dot(perm, rows, preferred_element_type=F32).astype(BF16)

    def y_copy(stage, u, ab):
        if stage == 0:
            return remote(r1s.at[u, ab], r1r.at[u, ab], r1_ssem.at[u, ab], r1_rsem.at[u, ab], first_mate[ab])
        if stage == 1:
            return remote(r2s.at[u, ab], r2r.at[u, ab], r2_ssem.at[u, ab], r2_rsem.at[u, ab], second_mate[ab])
        if stage == 2:
            ref = hid.at[u, pl.ds(4 * ab + 2 * keep_half[ab] + keep_quarter[ab], 1)]
            return remote(ref, ref, a1_ssem.at[u, ab], a1_rsem.at[u, ab], second_mate[ab])
        ref = hid.at[u, pl.ds(4 * ab + 2 * keep_half[ab], 2)]
        return remote(ref, ref, a2_ssem.at[u, ab], a2_rsem.at[u, ab], first_mate[ab])

    def y_recv(stage, u, ab):
        if stage < 2:
            y_copy(stage, u, ab).wait_recv()
        elif stage == 2:
            ref = hid.at[u, pl.ds(4 * ab + 2 * keep_half[ab] + 1 - keep_quarter[ab], 1)]
            remote(ref, ref, a1_ssem.at[u, ab], a1_rsem.at[u, ab], second_mate[ab]).wait_recv()
        else:
            ref = hid.at[u, pl.ds(4 * ab + 2 * (1 - keep_half[ab]), 2)]
            remote(ref, ref, a2_ssem.at[u, ab], a2_rsem.at[u, ab], first_mate[ab]).wait_recv()

    def stage_up(u):
        def block(b):
            at = pl.ds(pl.multiple_of(b * LANES, LANES), LANES)
            wa = jnp.concatenate([wg[0, :, at], wu[0, :, at]], axis=1)
            wb = jnp.concatenate([wg[role, :, at], wu[role, :, at]], axis=1)
            ya = jnp.dot(xc[u, :ua], wa, preferred_element_type=F32)
            yb = jnp.dot(xc[u, ua:], wb, preferred_element_type=F32)
            return jnp.concatenate([ya, yb], axis=0)

        for ab in range(2):

            def send(j, ab=ab):
                r1s[u, ab, j] = block(4 * ab + 2 * (1 - keep_half[ab]) + j).astype(BF16)

            loop(0, 2, send)
            y_copy(0, u, ab).start()
        for ab in range(2):

            def keep(j, ab=ab):
                part[u, ab, j] = block(4 * ab + 2 * keep_half[ab] + j)

            loop(0, 2, keep)

    def stage_sum(u):
        for ab in range(2):
            y_recv(0, u, ab)
            mine, other = keep_quarter[ab], 1 - keep_quarter[ab]
            r2s[u, ab] = (part[u, ab, other] + r1r[u, ab, other].astype(F32)).astype(BF16)
            y_copy(1, u, ab).start()
            part[u, ab, mine] = part[u, ab, mine] + r1r[u, ab, mine].astype(F32)

    def stage_act(u):
        for ab in range(2):
            y_recv(1, u, ab)
            v = part[u, ab, keep_quarter[ab]] + r2r[u, ab].astype(F32)
            gate, up = v[:, :LANES], v[:, LANES:]
            hidden = gate / (1.0 + jnp.exp(-gate)) * up
            hid[u, 4 * ab + 2 * keep_half[ab] + keep_quarter[ab]] = hidden.astype(BF16)
            y_copy(2, u, ab).start()

    def stage_pass(u):
        for ab in range(2):
            y_recv(2, u, ab)
            y_copy(3, u, ab).start()

    def stage_down(u):
        for ab in range(2):
            y_recv(3, u, ab)
        h = jnp.concatenate([hid[u, b] for b in range(8)], axis=1)
        res[u, :ua] = jnp.dot(h[:ua], wd[0], preferred_element_type=F32).astype(BF16)
        res[u, ua:] = jnp.dot(h[ua:], wd[role], preferred_element_type=F32).astype(BF16)

    def o_copy(r, s):
        xx, cc = slot_source(s)
        return remote(os_[r].at[s], or_[r].at[s], o_ssem.at[r, s], o_rsem.at[r, s], dev(y, z, xx, cc))

    def give_back(r):
        blocks = returns[r]
        nb = len(blocks)
        rr = room(cfg, nb)
        u0 = place_of[blocks[0]]
        block_of, local = layout(rr, nb)
        home = []
        for s in range(slots):
            at = jnp.where(local < cap, s * cap + local, ua + s * half + local - cap) + block_of * ur
            home.append(jnp.where(block_of < nb, at, -1))
        home = jnp.concatenate(home, axis=0)
        perm = jnp.where(home == iota((slots * rr, nb * ur), 1), 1.0, 0.0).astype(BF16)
        rows = res[u0 : u0 + nb].reshape(nb * ur, cols)
        spread = jnp.dot(perm, rows, preferred_element_type=F32)
        os_[r][...] = spread.reshape(slots, rr, cols).astype(BF16)
        loop(1, slots, lambda s: o_copy(r, s).start())
        or_[r][0] = spread[0:rr].astype(BF16)

    def combine(r):
        blocks = returns[r]
        nb = len(blocks)
        rr = room(cfg, nb)
        loop(1, slots, lambda s: o_copy(r, s).wait_recv())
        rows = joined(or_[r])
        for i, b in enumerate(blocks):
            n = entry[b]
            keys = slot_keys(rr, nb, i, True)
            w_hi = jnp.zeros((slots * rr, tb), F32)
            w_lo = jnp.zeros((slots * rr, tb), F32)
            for k in range(top):
                hit = codes[n, 0, k : k + 1, :] == keys
                w_hi = jnp.where(hit, codes[n, 1, k : k + 1, :], w_hi)
                w_lo = jnp.where(hit, codes[n, 2, k : k + 1, :], w_lo)
            dims = (((0,), (0,)), ((), ()))
            total = lax.dot_general(w_hi.astype(BF16), rows, dims, preferred_element_type=F32)
            acc[n] = total + lax.dot_general(w_lo.astype(BF16), rows, dims, preferred_element_type=F32)

    def c_copy(to_right, h, part_):
        i = (h - 1) if to_right else far + (h - 1)
        at = pl.ds(part_ * (tb // 2), tb // 2)
        return remote(
            csend.at[i, at], crecv.at[i, at], c_ssem.at[i, part_], c_rsem.at[i, part_],
            right if to_right else left,
        )

    def c_hop(to_right, h):
        d = (far - h + 1) if to_right else h - far
        i = (h - 1) if to_right else far + (h - 1)
        for part_ in range(2):
            at = slice(part_ * (tb // 2), (part_ + 1) * (tb // 2))
            v = acc[entry[d], at]
            if h > 1:
                c_copy(to_right, h - 1, part_).wait_recv()
                v = v + crecv[i - 1, at].astype(F32)
            csend[i, at] = v.astype(BF16)
            c_copy(to_right, h, part_).start()

    words = {
        "d": dispatch, "a": arrive, "u": stage_up, "s": stage_sum, "c": stage_act, "p": stage_pass, "e": stage_down,
        "o": give_back, "m": combine,
        "R": lambda h: c_hop(True, h), "L": lambda h: c_hop(False, h),
    }

    def run(text):
        for word in text.split():
            if word[0] == "r":
                relay(int(word[1]), int(word[2]))
            elif word[0] == "w":
                for ld in loads:
                    ld.wait()
            else:
                words[word[0]](int(word[1:]))

    for text in cfg["early"]:
        run(text)

    def step(n):
        for k, text in cfg["before"].items():

            @pl.when(n == k)
            def _(text=text):
                run(text)

        for lag, stage in enumerate((stage_up, stage_sum, stage_act, stage_pass, stage_down)):
            u = n - lag

            @pl.when((u >= cfg["begin"][lag]) & (u < units))
            def _(stage=stage, u=u):
                stage(u)

        for k, text in cfg["after"].items():

            @pl.when(n == k)
            def _(text=text):
                run(text)

    loop(cfg["begin"][0], units + 4, step)
    for text in cfg["late"]:
        run(text)
    for part_ in range(2):
        at = slice(part_ * (tb // 2), (part_ + 1) * (tb // 2))
        c_copy(True, far, part_).wait_recv()
        c_copy(False, far - 1, part_).wait_recv()
        v = acc[0, at] + crecv[far - 1, at].astype(F32) + crecv[nz - 2, at].astype(F32)
        out_ref[at, :] = v.astype(BF16)

    for to_right in (True, False):
        for piece in range(2):
            for h in range(1, z_hops(to_right, piece) + 1):
                z_copy(to_right, h, piece).wait_send()
            for h in range(1, (far if to_right else far - 1) + 1):
                c_copy(to_right, h, piece).wait_send()
    for g in range(ng):
        loop(1, slots, lambda s, g=g: x_copy(g, s).wait_send())
    for r in range(nr):
        loop(1, slots, lambda s, r=r: o_copy(r, s).wait_send())

    def sent_y(u):
        for ab in range(2):
            for stage in range(4):
                y_copy(stage, u, ab).wait_send()

    loop(0, units, sent_y)


def on_device(
    cfg, tokens, expert_ids, replica_choice, gate_weights, placement, capacity, w_gate, w_up, w_down
):
    nz, nx, nc, cap = cfg["nz"], cfg["nx"], cfg["nc"], cfg["cap"]
    groups, returns = cfg["groups"], cfg["returns"]
    tb, cols = tokens.shape
    top = expert_ids.shape[1]
    ff = w_gate.shape[-1]
    slots = nx * nc
    ur = slots * (cap + cap // 2)
    far = nz // 2
    units = nz
    vmem = pl.BlockSpec(memory_space=pltpu.VMEM)
    smem = pl.BlockSpec(memory_space=pltpu.SMEM)
    anywhere = pl.BlockSpec(memory_space=pl.ANY)
    dma = pltpu.SemaphoreType.DMA
    assert ff == 8 * LANES and top == 8

    def buf(*shape):
        return pltpu.VMEM(shape, BF16)

    scratch = [buf(2, cols, ff), buf(2, cols, ff), buf(2, ff, cols), dma((3,))]
    scratch += [buf(nz, tb + 2 * top, cols), pltpu.VMEM((nz, 3, top, tb), F32), dma((2, 2, far)), dma((2, 2, far))]
    scratch += [buf(slots, room(cfg, len(g)), cols) for _ in range(2) for g in groups]
    scratch += [dma((len(groups), slots)), dma((len(groups), slots)), buf(units, ur, cols)]
    scratch += [
        pltpu.VMEM((units, 2, 2, ur, 2 * LANES), F32),
        buf(units, 2, 2, ur, 2 * LANES), buf(units, 2, 2, ur, 2 * LANES),
        buf(units, 2, ur, 2 * LANES), buf(units, 2, ur, 2 * LANES),
        buf(units, 8, ur, LANES), buf(units, ur, cols),
    ]
    scratch += [dma((units, 2)) for _ in range(8)]
    scratch += [buf(slots, room(cfg, len(r)), cols) for _ in range(2) for r in returns]
    scratch += [dma((len(returns), slots)), dma((len(returns), slots))]
    scratch += [
        pltpu.VMEM((nz, tb, cols), F32), buf(nz - 1, tb, cols), buf(nz - 1, tb, cols),
        dma((nz - 1, 2)), dma((nz - 1, 2)),
    ]
    return pl.pallas_call(
        functools.partial(kernel, cfg),
        out_shape=jax.ShapeDtypeStruct((tb, cols), BF16),
        in_specs=[vmem, vmem, vmem, vmem, vmem, smem, vmem, anywhere, anywhere, anywhere],
        out_specs=vmem,
        scratch_shapes=scratch,
        compiler_params=pltpu.CompilerParams(
            collective_id=0, has_side_effects=True, vmem_limit_bytes=60 * 2**20
        ),
    )(
        tokens, expert_ids.T, replica_choice.T, gate_weights.T, placement.T, placement.T,
        capacity.reshape(1, -1), w_gate, w_up, w_down,
    )


def solution(mesh, cfg=None):
    return jax.shard_map(
        functools.partial(on_device, cfg or SIZES),
        mesh=mesh,
        in_specs=(
            P("expert", "dp"),
            P("expert", None),
            P("expert", None),
            P("expert", None),
            P(),
            P(),
            P("expert", None, "dp", None),
            P("expert", None, "dp", None),
            P("expert", None, None, "dp"),
        ),
        out_specs=P("expert", "dp"),
        check_vma=False,
    )
```

```python
import functools

import jax
import jax.numpy as jnp
from jax import lax
from jax.experimental import pallas as pl
from jax.experimental.pallas import tpu as pltpu
from jax.sharding import PartitionSpec as P

MESH = pl.DeviceIdType.MESH
F32 = jnp.float32
BF16 = jnp.bfloat16
I32 = jnp.int32
LANES = 128
CODE = 64
ALIGN = 8

SIZES = dict(
    nz=8, nx=4, nc=2, cap=12,
    groups=((0,), (1, -1), (2, -2), (3, -3), (4,)),
    order=(0, 1, -2, 4, 3, -3, 2, -1),
    returns=((0, 1), (-2, 4), (3,), (-3,), (2,), (-1,)),
    early=(
        "d0 r10 r11 d1", "w a0 u0 r20", "s0 r21 d2 c0", "r30 a1 u1 r31", "d3 p0 s1 r40", "a2 u2 r41 d4", "c1 s2",
    ),
    begin=(3, 3, 2, 1, 0),
    before={3: "a4", 4: "a3"},
    after={5: "o0", 7: "o1 m0", 8: "o2 m1 R1", 9: "o3 m2 R2", 10: "o4 m3 L1", 11: "o5 L2"},
    late=("m4 R3 m5", "L3 R4"),
)


def room(cfg, blocks):
    return -(-blocks * (cfg["cap"] + cfg["cap"] // 2) // ALIGN) * ALIGN


def kernel(cfg, *refs):
    groups, order, returns = cfg["groups"], cfg["order"], cfg["returns"]
    ng, nr = len(groups), len(returns)
    refs = list(refs)

    def take(n):
        out = refs[:n]
        del refs[:n]
        return out

    tok_ref, ids_ref, rep_ref, gw_ref, place_ref, place_s, cap_ref, wg_hbm, wu_hbm, wd_hbm = take(10)
    (out_ref,) = take(1)
    wg, wu, wd, w_sem = take(4)
    tokg, codes, z_ssem, z_rsem = take(4)
    xs, xr = take(ng), take(ng)
    x_ssem, x_rsem, xc = take(3)
    part, r1s, r1r, r2s, r2r, hid, res = take(7)
    r1_ssem, r1_rsem, r2_ssem, r2_rsem, a1_ssem, a1_rsem, a2_ssem, a2_rsem = take(8)
    os_, or_ = take(nr), take(nr)
    o_ssem, o_rsem = take(2)
    acc, csend, crecv, c_ssem, c_rsem = take(5)
    assert not refs

    nz, nx, nc, cap = cfg["nz"], cfg["nx"], cfg["nc"], cfg["cap"]
    half = cap // 2
    each = cap + half
    experts = nz * nx * nc
    hot = place_ref.shape[1]
    top = ids_ref.shape[0]
    tb, cols = tok_ref.shape
    far = nz // 2
    slots = nx * nc
    ua, ub = slots * cap, slots * half
    ur = ua + ub
    units = nz
    flat = [b for g in groups for b in g]
    entry = {b: i for i, b in enumerate(flat)}
    place_of = {b: i for i, b in enumerate(order)}

    y = lax.axis_index("dp")
    e = lax.axis_index("expert")
    z = e // slots
    x = (e // nc) % nx
    c = e % nc

    def dev(yy, zz, xx, cc):
        return (yy, (zz * nx + xx) * nc + cc)

    right = dev(y, lax.rem(z + 1, nz), x, c)
    left = dev(y, lax.rem(z + nz - 1, nz), x, c)
    odd, high = y % 2, y // 2
    mate1 = dev(y + 1 - 2 * odd, z, x, c)
    mate2 = dev(3 - y, z, x, c)
    first_mate = (mate1, mate2)
    second_mate = (mate2, mate1)
    keep_half = ((odd + high) % 2, high)
    keep_quarter = (high, odd)

    def slot_dest(s):
        dx, dc = s // nc, s % nc
        return lax.rem(x + dx, nx), lax.rem(c + dc, nc)

    def slot_source(s):
        dx, dc = s // nc, s % nc
        return lax.rem(x + nx - dx, nx), lax.rem(c + nc - dc, nc)

    loads = [
        pltpu.make_async_copy(h.at[0], v, w_sem.at[i])
        for i, (h, v) in enumerate(((wg_hbm, wg), (wu_hbm, wu), (wd_hbm, wd)))
    ]
    for ld in loads:
        ld.start()

    barrier = pltpu.get_barrier_semaphore()
    peers = [right, left, mate1, mate2]
    for s in range(1, slots):
        peers.append(dev(y, z, *slot_dest(s)))
    for peer in peers:
        pl.semaphore_signal(barrier, inc=1, device_id=peer, device_id_type=MESH)

    def remote(src, dst, ssem, rsem, device):
        return pltpu.make_async_remote_copy(
            src_ref=src, dst_ref=dst, send_sem=ssem, recv_sem=rsem,
            device_id=device, device_id_type=MESH,
        )

    pieces = ((0, tb // 2), (tb // 2, tb // 2 + 2 * top))

    def z_hops(to_right, piece):
        return far if to_right == (piece == 0) else far - 1

    def z_copy(to_right, h, piece):
        sign = -1 if to_right else 1

        def at(hops):
            return entry[far if hops == far else sign * hops]

        rows = pl.ds(*pieces[piece])
        source = tok_ref.at[rows] if (h == 1 and piece == 0) else tokg.at[at(h - 1), rows]
        d = 0 if to_right else 1
        return remote(
            source, tokg.at[at(h), rows], z_ssem.at[d, piece, h - 1], z_rsem.at[d, piece, h - 1],
            right if to_right else left,
        )

    def z_start(h, piece):
        for to_right in (True, False):
            if h <= z_hops(to_right, piece):
                z_copy(to_right, h, piece).start()

    def relay(h, piece):
        for to_right in (True, False):
            if h <= z_hops(to_right, piece):
                z_copy(to_right, h, piece).wait_recv()
                if h < z_hops(to_right, piece):
                    z_copy(to_right, h + 1, piece).start()


    def iota(shape, dim):
        return lax.broadcasted_iota(I32, shape, dim)

    def column(row):
        n = row.shape[1]
        return jnp.sum(jnp.where(iota((n, n), 0) == iota((n, n), 1), row, 0), axis=1, keepdims=True)

    reps = experts + hot
    hot_col = column(place_ref[0:1, :])
    host_col = column(place_ref[1:2, :])
    cap_col = column(cap_ref[...])
    r_iota = iota((reps, tb), 0)
    j_iota = iota((hot, tb), 0)
    targets = []
    chosen = jnp.zeros((reps, tb), F32)
    for k in range(top):
        idk = ids_ref[k : k + 1, :]
        j = jnp.sum(jnp.where(hot_col == idk, j_iota, 0), axis=0, keepdims=True)
        t = jnp.where(rep_ref[k : k + 1, :] == 1, experts + j, idk)
        targets.append(t)
        chosen = chosen + jnp.where(r_iota == t, 1.0, 0.0)
    earlier = jnp.where(iota((tb, tb), 0) < iota((tb, tb), 1), 1.0, 0.0).astype(BF16)
    rank = jnp.dot(chosen.astype(BF16), earlier, preferred_element_type=F32).astype(I32)
    own_code = r_iota[:experts] * CODE + rank[:experts]
    rank_c = rank[experts:]
    copy_code = jnp.where(
        rank_c < half,
        hot_col * CODE + cap + rank_c,
        host_col * CODE + (cap - half) + rank_c,
    )
    code = jnp.concatenate([own_code, copy_code], axis=0)
    code = jnp.where(rank < cap_col, code, -CODE)
    rows = [
        jnp.sum(jnp.where(r_iota == targets[k], code, 0), axis=0, keepdims=True) for k in range(top)
    ]
    code = jnp.concatenate(rows, axis=0)
    whose = jnp.right_shift(code, 6)
    gw = gw_ref[...]
    gw_hi = gw.astype(BF16)
    gw_lo = (gw - gw_hi.astype(F32)).astype(BF16)
    tail = (whose.astype(F32).astype(BF16), (code - whose * CODE).astype(F32).astype(BF16), gw_hi, gw_lo)
    tokg[0, tb:] = jnp.zeros((2 * top, cols), BF16)
    for i, t in enumerate(tail):
        tokg[0, tb : tb + top, i * tb : (i + 1) * tb] = t
    tokg[0, :tb] = tok_ref[...]
    pl.semaphore_wait(barrier, len(peers))
    z_start(1, 0)
    z_start(1, 1)

    role = jnp.int32(0)
    for j in range(hot):
        role = jnp.maximum(role, jnp.where(place_s[1, j] == e, 1, 0))

    def read_codes(n):
        t = tokg[n, tb : tb + top, 0 : 4 * tb].astype(F32)
        codes[n, 0] = t[:, :tb] * CODE + t[:, tb : 2 * tb]
        codes[n, 1] = t[:, 2 * tb : 3 * tb]
        codes[n, 2] = t[:, 3 * tb :]

    def layout(rr, blocks):
        p = iota((rr, 1), 0)
        block_of = jnp.zeros((rr, 1), I32)
        for i in range(1, blocks + 1):
            block_of = block_of + jnp.where(p >= i * each, 1, 0)
        return block_of, p - block_of * each

    def slot_keys(rr, blocks, i, source):
        block_of, local = layout(rr, blocks)
        keys = []
        for s in range(slots):
            xx, cc = slot_dest(s)
            key = ((z * nx + xx) * nc + cc) * CODE + local
            keys.append(jnp.where(block_of == i, key, -2))
        return jnp.concatenate(keys, axis=0).astype(F32)

    def x_copy(g, s):
        xx, cc = slot_dest(s)
        return remote(xs[g].at[s], xr[g].at[s], x_ssem.at[g, s], x_rsem.at[g, s], dev(y, z, xx, cc))

    def loop(lo, hi, f):
        def body(i, carry):
            f(i)
            return carry

        lax.fori_loop(lo, hi, body, 0)

    def dispatch(g):
        blocks = groups[g]
        nb = len(blocks)
        rr = room(cfg, nb)
        n0 = entry[blocks[0]]
        sel = []
        for i in range(nb):
            read_codes(n0 + i)
            keys = slot_keys(rr, nb, i, False)
            hit = jnp.zeros((slots * rr, tb), jnp.bool_)
            for k in range(top):
                hit = hit | (codes[n0 + i, 0, k : k + 1, :] == keys)
            sel.append(jnp.where(hit, 1.0, 0.0).astype(BF16))
        sel = jnp.concatenate(sel, axis=1)
        toks = tokg[n0 : n0 + nb, :tb].reshape(nb * tb, cols)
        picked = jnp.dot(sel, toks, preferred_element_type=F32)
        xs[g][...] = picked.reshape(slots, rr, cols).astype(BF16)
        loop(1, slots, lambda s: x_copy(g, s).start())
        xr[g][0] = picked[0:rr].astype(BF16)

    def joined(ref):
        return ref[...].astype(F32).reshape(slots * ref.shape[1], cols).astype(BF16)

    def unit_rows(rr, i):
        p = iota((ur, 1), 0)
        s = jnp.zeros((ur, 1), I32)
        for j in range(1, slots):
            s = s + jnp.where(p >= j * cap, 1, 0) * jnp.where(p < ua, 1, 0)
            s = s + jnp.where(p >= ua + j * half, 1, 0)
        local = jnp.where(p < ua, p - s * cap, p - ua - s * half + cap)
        return s * rr + i * each + local

    def arrive(g):
        blocks = groups[g]
        rr = room(cfg, len(blocks))
        loop(1, slots, lambda s: x_copy(g, s).wait_recv())
        rows = joined(xr[g])
        for i, b in enumerate(blocks):
            perm = jnp.where(unit_rows(rr, i) == iota((ur, slots * rr), 1), 1.0, 0.0).astype(BF16)
            xc[place_of[b]] = jnp.dot(perm, rows, preferred_element_type=F32).astype(BF16)

    def y_copy(stage, u, ab):
        if stage == 0:
            return remote(r1s.at[u, ab], r1r.at[u, ab], r1_ssem.at[u, ab], r1_rsem.at[u, ab], first_mate[ab])
        if stage == 1:
            return remote(r2s.at[u, ab], r2r.at[u, ab], r2_ssem.at[u, ab], r2_rsem.at[u, ab], second_mate[ab])
        if stage == 2:
            ref = hid.at[u, pl.ds(4 * ab + 2 * keep_half[ab] + keep_quarter[ab], 1)]
            return remote(ref, ref, a1_ssem.at[u, ab], a1_rsem.at[u, ab], second_mate[ab])
        ref = hid.at[u, pl.ds(4 * ab + 2 * keep_half[ab], 2)]
        return remote(ref, ref, a2_ssem.at[u, ab], a2_rsem.at[u, ab], first_mate[ab])

    def y_recv(stage, u, ab):
        if stage < 2:
            y_copy(stage, u, ab).wait_recv()
        elif stage == 2:
            ref = hid.at[u, pl.ds(4 * ab + 2 * keep_half[ab] + 1 - keep_quarter[ab], 1)]
            remote(ref, ref, a1_ssem.at[u, ab], a1_rsem.at[u, ab], second_mate[ab]).wait_recv()
        else:
            ref = hid.at[u, pl.ds(4 * ab + 2 * (1 - keep_half[ab]), 2)]
            remote(ref, ref, a2_ssem.at[u, ab], a2_rsem.at[u, ab], first_mate[ab]).wait_recv()

    def stage_up(u):
        def block(b):
            at = pl.ds(pl.multiple_of(b * LANES, LANES), LANES)
            wa = jnp.concatenate([wg[0, :, at], wu[0, :, at]], axis=1)
            wb = jnp.concatenate([wg[role, :, at], wu[role, :, at]], axis=1)
            ya = jnp.dot(xc[u, :ua], wa, preferred_element_type=F32)
            yb = jnp.dot(xc[u, ua:], wb, preferred_element_type=F32)
            return jnp.concatenate([ya, yb], axis=0)

        for ab in range(2):

            def send(j, ab=ab):
                r1s[u, ab, j] = block(4 * ab + 2 * (1 - keep_half[ab]) + j).astype(BF16)

            loop(0, 2, send)
            y_copy(0, u, ab).start()
        for ab in range(2):

            def keep(j, ab=ab):
                part[u, ab, j] = block(4 * ab + 2 * keep_half[ab] + j)

            loop(0, 2, keep)

    def stage_sum(u):
        for ab in range(2):
            y_recv(0, u, ab)
            mine, other = keep_quarter[ab], 1 - keep_quarter[ab]
            r2s[u, ab] = (part[u, ab, other] + r1r[u, ab, other].astype(F32)).astype(BF16)
            y_copy(1, u, ab).start()
            part[u, ab, mine] = part[u, ab, mine] + r1r[u, ab, mine].astype(F32)

    def stage_act(u):
        for ab in range(2):
            y_recv(1, u, ab)
            v = part[u, ab, keep_quarter[ab]] + r2r[u, ab].astype(F32)
            gate, up = v[:, :LANES], v[:, LANES:]
            hidden = gate / (1.0 + jnp.exp(-gate)) * up
            hid[u, 4 * ab + 2 * keep_half[ab] + keep_quarter[ab]] = hidden.astype(BF16)
            y_copy(2, u, ab).start()

    def stage_pass(u):
        for ab in range(2):
            y_recv(2, u, ab)
            y_copy(3, u, ab).start()

    def stage_down(u):
        for ab in range(2):
            y_recv(3, u, ab)
        h = jnp.concatenate([hid[u, b] for b in range(8)], axis=1)
        res[u, :ua] = jnp.dot(h[:ua], wd[0], preferred_element_type=F32).astype(BF16)
        res[u, ua:] = jnp.dot(h[ua:], wd[role], preferred_element_type=F32).astype(BF16)

    def o_copy(r, s):
        xx, cc = slot_source(s)
        return remote(os_[r].at[s], or_[r].at[s], o_ssem.at[r, s], o_rsem.at[r, s], dev(y, z, xx, cc))

    def give_back(r):
        blocks = returns[r]
        nb = len(blocks)
        rr = room(cfg, nb)
        u0 = place_of[blocks[0]]
        block_of, local = layout(rr, nb)
        home = []
        for s in range(slots):
            at = jnp.where(local < cap, s * cap + local, ua + s * half + local - cap) + block_of * ur
            home.append(jnp.where(block_of < nb, at, -1))
        home = jnp.concatenate(home, axis=0)
        perm = jnp.where(home == iota((slots * rr, nb * ur), 1), 1.0, 0.0).astype(BF16)
        rows = res[u0 : u0 + nb].reshape(nb * ur, cols)
        spread = jnp.dot(perm, rows, preferred_element_type=F32)
        os_[r][...] = spread.reshape(slots, rr, cols).astype(BF16)
        loop(1, slots, lambda s: o_copy(r, s).start())
        or_[r][0] = spread[0:rr].astype(BF16)

    def combine(r):
        blocks = returns[r]
        nb = len(blocks)
        rr = room(cfg, nb)
        loop(1, slots, lambda s: o_copy(r, s).wait_recv())
        rows = joined(or_[r])
        for i, b in enumerate(blocks):
            n = entry[b]
            keys = slot_keys(rr, nb, i, True)
            w_hi = jnp.zeros((slots * rr, tb), F32)
            w_lo = jnp.zeros((slots * rr, tb), F32)
            for k in range(top):
                hit = codes[n, 0, k : k + 1, :] == keys
                w_hi = jnp.where(hit, codes[n, 1, k : k + 1, :], w_hi)
                w_lo = jnp.where(hit, codes[n, 2, k : k + 1, :], w_lo)
            dims = (((0,), (0,)), ((), ()))
            total = lax.dot_general(w_hi.astype(BF16), rows, dims, preferred_element_type=F32)
            acc[n] = total + lax.dot_general(w_lo.astype(BF16), rows, dims, preferred_element_type=F32)

    def c_copy(to_right, h, part_):
        i = (h - 1) if to_right else far + (h - 1)
        at = pl.ds(part_ * (tb // 2), tb // 2)
        return remote(
            csend.at[i, at], crecv.at[i, at], c_ssem.at[i, part_], c_rsem.at[i, part_],
            right if to_right else left,
        )

    def c_hop(to_right, h):
        d = (far - h + 1) if to_right else h - far
        i = (h - 1) if to_right else far + (h - 1)
        for part_ in range(2):
            at = slice(part_ * (tb // 2), (part_ + 1) * (tb // 2))
            v = acc[entry[d], at]
            if h > 1:
                c_copy(to_right, h - 1, part_).wait_recv()
                v = v + crecv[i - 1, at].astype(F32)
            csend[i, at] = v.astype(BF16)
            c_copy(to_right, h, part_).start()

    words = {
        "d": dispatch, "a": arrive, "u": stage_up, "s": stage_sum, "c": stage_act, "p": stage_pass, "e": stage_down,
        "o": give_back, "m": combine,
        "R": lambda h: c_hop(True, h), "L": lambda h: c_hop(False, h),
    }

    def run(text):
        for word in text.split():
            if word[0] == "r":
                relay(int(word[1]), int(word[2]))
            elif word[0] == "w":
                for ld in loads:
                    ld.wait()
            else:
                words[word[0]](int(word[1:]))

    for text in cfg["early"]:
        run(text)

    def step(n):
        for k, text in cfg["before"].items():

            @pl.when(n == k)
            def _(text=text):
                run(text)

        for lag, stage in enumerate((stage_up, stage_sum, stage_act, stage_pass, stage_down)):
            u = n - lag

            @pl.when((u >= cfg["begin"][lag]) & (u < units))
            def _(stage=stage, u=u):
                stage(u)

        for k, text in cfg["after"].items():

            @pl.when(n == k)
            def _(text=text):
                run(text)

    loop(cfg["begin"][0], units + 4, step)
    for text in cfg["late"]:
        run(text)
    for part_ in range(2):
        at = slice(part_ * (tb // 2), (part_ + 1) * (tb // 2))
        c_copy(True, far, part_).wait_recv()
        c_copy(False, far - 1, part_).wait_recv()
        v = acc[0, at] + crecv[far - 1, at].astype(F32) + crecv[nz - 2, at].astype(F32)
        out_ref[at, :] = v.astype(BF16)

    for to_right in (True, False):
        for piece in range(2):
            for h in range(1, z_hops(to_right, piece) + 1):
                z_copy(to_right, h, piece).wait_send()
            for h in range(1, (far if to_right else far - 1) + 1):
                c_copy(to_right, h, piece).wait_send()
    for g in range(ng):
        loop(1, slots, lambda s, g=g: x_copy(g, s).wait_send())
    for r in range(nr):
        loop(1, slots, lambda s, r=r: o_copy(r, s).wait_send())

    def sent_y(u):
        for ab in range(2):
            for stage in range(4):
                y_copy(stage, u, ab).wait_send()

    loop(0, units, sent_y)


def on_device(
    cfg, tokens, expert_ids, replica_choice, gate_weights, placement, capacity, w_gate, w_up, w_down
):
    nz, nx, nc, cap = cfg["nz"], cfg["nx"], cfg["nc"], cfg["cap"]
    groups, returns = cfg["groups"], cfg["returns"]
    tb, cols = tokens.shape
    top = expert_ids.shape[1]
    ff = w_gate.shape[-1]
    slots = nx * nc
    ur = slots * (cap + cap // 2)
    far = nz // 2
    units = nz
    vmem = pl.BlockSpec(memory_space=pltpu.VMEM)
    smem = pl.BlockSpec(memory_space=pltpu.SMEM)
    anywhere = pl.BlockSpec(memory_space=pl.ANY)
    dma = pltpu.SemaphoreType.DMA
    assert ff == 8 * LANES and top == 8

    def buf(*shape):
        return pltpu.VMEM(shape, BF16)

    scratch = [buf(2, cols, ff), buf(2, cols, ff), buf(2, ff, cols), dma((3,))]
    scratch += [buf(nz, tb + 2 * top, cols), pltpu.VMEM((nz, 3, top, tb), F32), dma((2, 2, far)), dma((2, 2, far))]
    scratch += [buf(slots, room(cfg, len(g)), cols) for _ in range(2) for g in groups]
    scratch += [dma((len(groups), slots)), dma((len(groups), slots)), buf(units, ur, cols)]
    scratch += [
        pltpu.VMEM((units, 2, 2, ur, 2 * LANES), F32),
        buf(units, 2, 2, ur, 2 * LANES), buf(units, 2, 2, ur, 2 * LANES),
        buf(units, 2, ur, 2 * LANES), buf(units, 2, ur, 2 * LANES),
        buf(units, 8, ur, LANES), buf(units, ur, cols),
    ]
    scratch += [dma((units, 2)) for _ in range(8)]
    scratch += [buf(slots, room(cfg, len(r)), cols) for _ in range(2) for r in returns]
    scratch += [dma((len(returns), slots)), dma((len(returns), slots))]
    scratch += [
        pltpu.VMEM((nz, tb, cols), F32), buf(nz - 1, tb, cols), buf(nz - 1, tb, cols),
        dma((nz - 1, 2)), dma((nz - 1, 2)),
    ]
    return pl.pallas_call(
        functools.partial(kernel, cfg),
        out_shape=jax.ShapeDtypeStruct((tb, cols), BF16),
        in_specs=[vmem, vmem, vmem, vmem, vmem, smem, vmem, anywhere, anywhere, anywhere],
        out_specs=vmem,
        scratch_shapes=scratch,
        compiler_params=pltpu.CompilerParams(
            collective_id=0, has_side_effects=True, vmem_limit_bytes=60 * 2**20
        ),
    )(
        tokens, expert_ids.T, replica_choice.T, gate_weights.T, placement.T, placement.T,
        capacity.reshape(1, -1), w_gate, w_up, w_down,
    )


def solution(mesh, cfg=None):
    return jax.shard_map(
        functools.partial(on_device, cfg or SIZES),
        mesh=mesh,
        in_specs=(
            P("expert", "dp"),
            P("expert", None),
            P("expert", None),
            P("expert", None),
            P(),
            P(),
            P("expert", None, "dp", None),
            P("expert", None, "dp", None),
            P("expert", None, None, "dp"),
        ),
        out_specs=P("expert", "dp"),
        check_vma=False,
    )
```
